256 devices in a mesh: lat: 16 (over x_lo, y, core), lon: 16 (over x_hi, z).
Axes of the slice: x: 4 (x_hi: 2, x_lo: 2; x = x_hi * 2 + x_lo), y: 4, z: 8, core: 2. Of those that a mesh axis runs over, the one named last changes fastest.
Arguments:
- tokens: bfloat16 [2, 96, 192, 1024], P(None, 'lat', 'lon'), may hold values from -6 to 6
- layer_norm_gain: float32 [1024], replicated, may hold values from 0.5 to 1.5
- layer_norm_bias: float32 [1024], replicated, may hold values from -3 to 3
- w_qkv: bfloat16 [1024, 1536], replicated, may hold values from -2 to 2
- w_out: bfloat16 [512, 1024], replicated, may hold values from -0.25 to 0.25
- output_cotangent: bfloat16 [2, 96, 192, 1024], P(None, 'lat', 'lon'), may hold values from -6 to 6
Outputs:
- output: bfloat16 [2, 96, 192, 1024], P(None, 'lat', 'lon')
- token_gradient: bfloat16 [2, 96, 192, 1024], P(None, 'lat', 'lon')
- d_qkv: float32 [1024, 1536], P(('lat', 'lon'))
- d_out: float32 [512, 1024], P(None, ('lat', 'lon'))
- gain_gradient_scaled: float32 [1024], P(('lat', 'lon'))
- d_bias: float32 [1024], P(('lat', 'lon'))
The draws below stay inside these ranges and needn't reach their ends.
All inputs are finite; a program needn't handle non-finite values.
Results may differ from the reference program's by a relative error of at most 0.0093.
Values may be sent and summed in bfloat16 or wider, within the bound.
A program may use at most 64 MiB of HBM per device.

```python
import math
import jax
import jax.numpy as jnp
from jax import lax

D = 1024
HEADS = 8
HDIM = 64
WLAT = 6
WLON = 12
LEV = 2
HD = 512
NLAT = 96
NLON = 192
TOKENS = 36864


def draw_w_qkv(key, part):
    inner_width = HEADS * HDIM
    first_key = jax.random.fold_in(jax.random.fold_in(key, 11), 0)
    base = jax.random.normal(first_key, (D, 3 * inner_width), jnp.float32) / math.sqrt(D)
    result = base
    return jnp.clip(result, -2.0, 2.0).astype(jnp.bfloat16)


def with_spikes(entries, rng, source, target, blocks, factor):
    owner, partner = [(jnp.arange(entries.shape[position]) // (entries.shape[position] // blocks)).reshape([-1 if axis == position else 1 for axis in range(entries.ndim)]) for position in (source, target)]
    chosen = jax.random.permutation(rng, blocks)[partner]
    strong = (owner == chosen) | (owner == (partner + blocks // 2) % blocks)
    return jnp.where(strong, factor * entries, entries)


def block_levels(rng, dims, cuts, least, largest):
    def one(axis_at, blocks):
        draws = jax.random.uniform(jax.random.fold_in(jax.random.fold_in(rng, 6), axis_at), (blocks,), jnp.float32, least / len(cuts), largest / len(cuts))
        return jnp.repeat(jnp.exp(draws), dims[axis_at] // blocks).reshape((-1,) + (1,) * (len(dims) - axis_at - 1))

    loudness = one(*cuts[0])
    for cut in cuts[1:]:
        loudness = loudness * one(*cut)
    return loudness


def centred(own_key, shape, width, bound, cuts=(), held_as=jnp.bfloat16):
    values = jax.random.normal(own_key, shape, jnp.float32) * width
    if len(cuts) > 0:
        values = block_levels(own_key, shape, cuts, -0.22, 0.18) * values
    return jnp.clip(values, min=-bound, max=bound).astype(held_as)


def bell_draw_with(rng, extent, spread, limit, shards, heavy, dtype=jnp.bfloat16):
    drawn = spread * jax.random.normal(rng, extent, jnp.float32)
    if shards:
        drawn = drawn * block_levels(rng, extent, shards, -0.22, 0.18)
    return jnp.clip(with_spikes(drawn, jax.random.fold_in(rng, 3), *heavy), -limit, limit).astype(dtype)


def setup_inputs(seed: int = 0) -> dict:
    key_list = jax.random.split(jax.random.key(seed), 7)
    return {
        "tokens": centred(key_list[0], (LEV, NLAT, NLON, D), 1.0, 6.0, ((1, 16), (2, 16))),
        "layer_norm_gain": jnp.clip(1.0 + 0.1 * jax.random.normal(key_list[1], (D,), jnp.float32), 0.5, 1.5),
        "layer_norm_bias": centred(key_list[2], (D,), 0.5, 3.0, (), jnp.float32),
        "w_qkv": draw_w_qkv(jax.random.fold_in(key_list[6], 71), 0),
        "w_out": centred(key_list[4], (HD, D), HD ** -0.5, 0.25),
        "output_cotangent": bell_draw_with(key_list[5], (LEV, NLAT, NLON, D), 1.0, 6.0, ((1, 16), (2, 16)), (2, 3, 16, 2.0)),
    }


def windows(grid_data, win_rows):
    levels, row_total, col_total, channels = grid_data.shape
    grid_data = grid_data.reshape(levels, row_total // win_rows, win_rows, col_total // WLON, WLON, channels)
    grid_data = grid_data.transpose(1, 3, 0, 2, 4, 5)
    return grid_data.reshape(-1, levels * win_rows * WLON, channels)

def from_windows(win_data, levels, row_total, col_total, win_rows):
    channels = win_data.shape[-1]
    grid_data = win_data.reshape(row_total // win_rows, col_total // WLON, levels, win_rows, WLON, channels)
    grid_data = grid_data.transpose(2, 0, 3, 1, 4, 5)
    return grid_data.reshape(levels, row_total, col_total, channels)

def attend(queries, key_part, value_part, grad_att, key_valid):
    score_scale = queries.shape[-1] ** (-0.5)
    query_wide = queries.astype(jnp.float32)
    key_wide = key_part.astype(jnp.float32)
    value_wide = value_part.astype(jnp.float32)
    grad_wide = grad_att.astype(jnp.float32)
    scores = jnp.einsum('nqhd,nkhd->nhqk', query_wide, key_wide) * score_scale
    scores = jnp.where(key_valid[:, None, None, :], scores, -1e+30)
    row_max = lax.optimization_barrier(jnp.max(scores, axis=-1, keepdims=True))
    exp_scores = jnp.exp(scores - row_max)
    probabilities = exp_scores / lax.optimization_barrier(jnp.sum(exp_scores, axis=-1, keepdims=True))
    probs_low = lax.optimization_barrier(probabilities.astype(jnp.bfloat16)).astype(jnp.float32)
    attended = jnp.einsum('nhqk,nkhd->nqhd', probs_low, value_wide).astype(jnp.bfloat16)
    grad_prob = jnp.einsum('nqhd,nkhd->nhqk', grad_wide, value_wide)
    row_inner = lax.optimization_barrier(jnp.sum(probabilities * grad_prob, axis=-1, keepdims=True))
    grad_score = lax.optimization_barrier((probabilities * (grad_prob - row_inner)).astype(jnp.bfloat16)).astype(jnp.float32)
    grad_query = (jnp.einsum('nhqk,nkhd->nqhd', grad_score, key_wide) * score_scale).astype(jnp.bfloat16)
    grad_key = jnp.einsum('nhqk,nqhd->nkhd', grad_score, query_wide) * score_scale
    grad_value = jnp.einsum('nhqk,nqhd->nkhd', probs_low, grad_wide)
    return (attended, grad_query, grad_key, grad_value)

def reference(tokens, layer_norm_gain, layer_norm_bias, w_qkv, w_out, output_cotangent):
    half_lat = WLAT // 2
    half_lon = WLON // 2
    norm_factor = 1.0 / math.sqrt(TOKENS)
    tokens_wide = tokens.astype(jnp.float32)
    average = lax.optimization_barrier(jnp.mean(tokens_wide, axis=-1, keepdims=True))
    centered_input = tokens_wide - average
    inverse_deviation = lax.rsqrt(lax.optimization_barrier(jnp.mean(centered_input * centered_input, axis=-1, keepdims=True)) + 1e-05)
    standardized_input = centered_input * inverse_deviation
    normalized_tokens = (standardized_input * layer_norm_gain + layer_norm_bias).astype(jnp.bfloat16)
    flat_normed = normalized_tokens.reshape(-1, D)
    projected = jnp.dot(flat_normed, w_qkv, preferred_element_type=jnp.float32).astype(jnp.bfloat16)
    grad_flat = output_cotangent.reshape(-1, D)
    grad_att = jnp.dot(grad_flat, w_out.T, preferred_element_type=jnp.float32).astype(jnp.bfloat16)
    stacked = jnp.concatenate([projected, grad_att], axis=-1).reshape(LEV, NLAT, NLON, 4 * HD)
    stacked = jnp.pad(stacked, ((0, 0), (half_lat, half_lat), (half_lon, half_lon), (0, 0)))
    row_index = jnp.arange(NLAT + WLAT)
    row_ok = jnp.logical_and(row_index >= half_lat, row_index < NLAT + half_lat).astype(jnp.float32)
    col_index = jnp.arange(NLON + WLON)
    col_ok = jnp.logical_and(col_index >= half_lon, col_index < NLON + half_lon).astype(jnp.float32)
    valid_grid = row_ok.reshape(1, NLAT + WLAT, 1, 1) * col_ok.reshape(1, 1, NLON + WLON, 1)
    valid_grid = jnp.broadcast_to(valid_grid, (LEV, NLAT + WLAT, NLON + WLON, 1))
    lat_groups = (NLAT + WLAT) // WLAT
    lon_groups = (NLON + WLON) // WLON
    win_data = windows(stacked, WLAT)
    win_len = win_data.shape[1]
    win_data = win_data.reshape(lat_groups, lon_groups, win_len, 4 * HD)
    win_valid = (windows(valid_grid, WLAT)[..., 0] > 0.5).reshape(lat_groups, lon_groups, win_len)

    def one_band(operands):
        block, block_valid = operands
        parts = block.reshape(lon_groups, win_len, 4, HEADS, HDIM)
        attended, grad_query, grad_key, grad_value = attend(parts[:, :, 0], parts[:, :, 1], parts[:, :, 2], parts[:, :, 3], block_valid)
        pieces = [attended, grad_query, grad_key.astype(jnp.bfloat16), grad_value.astype(jnp.bfloat16)]
        return jnp.concatenate([piece.reshape(lon_groups, win_len, HD) for piece in pieces], axis=-1)
    results = lax.map(one_band, (win_data, win_valid))
    results = from_windows(results.reshape(lat_groups * lon_groups, win_len, 4 * HD), LEV, NLAT + WLAT, NLON + WLON, WLAT)
    results = results[:, half_lat:half_lat + NLAT, half_lon:half_lon + NLON]
    attended = results[..., :HD].reshape(-1, HD)
    grad_proj = results[..., HD:].reshape(-1, 3 * HD)
    mixed = jnp.dot(attended, w_out, preferred_element_type=jnp.float32).reshape(tokens_wide.shape)
    y_out = (tokens_wide + mixed).astype(jnp.bfloat16)
    d_out = jnp.dot(attended.T, grad_flat, preferred_element_type=jnp.float32) * norm_factor
    d_qkv = jnp.dot(flat_normed.T, grad_proj, preferred_element_type=jnp.float32) * norm_factor
    gradient_of_normalized = jnp.dot(grad_proj, w_qkv.T, preferred_element_type=jnp.float32).reshape(tokens_wide.shape)
    gain_gradient_scaled = lax.optimization_barrier(jnp.sum(gradient_of_normalized * standardized_input, axis=(0, 1, 2))) * norm_factor
    d_bias = lax.optimization_barrier(jnp.sum(gradient_of_normalized, axis=(0, 1, 2))) * norm_factor
    gradient_of_standardized = gradient_of_normalized * layer_norm_gain
    first_moment_term = lax.optimization_barrier(jnp.mean(gradient_of_standardized, axis=-1, keepdims=True))
    second_moment_term = lax.optimization_barrier(jnp.mean(gradient_of_standardized * standardized_input, axis=-1, keepdims=True))
    token_gradient = (output_cotangent.astype(jnp.float32) + (gradient_of_standardized - first_moment_term - standardized_input * second_moment_term) * inverse_deviation).astype(jnp.bfloat16)
    return (y_out, token_gradient, d_qkv, d_out, gain_gradient_scaled, d_bias)
```

```python
import math

import jax
import jax.numpy as jnp
from jax import lax
from jax.experimental import pallas as pl
from jax.experimental.pallas import tpu as pltpu
from jax.sharding import PartitionSpec as P

MESH = pl.DeviceIdType.MESH
BF = jnp.bfloat16
F32 = jnp.float32

D = 1024
HD = 512
TOK = 144
QUARTER = 36
NX, NY, NZ = 4, 4, 8
LAT, LON = 16, 16
PHASES = 2
WIDTH = 1024


def dot(a, b):
    return jnp.dot(a, b, preferred_element_type=F32)


def dot_nt(a, b):
    return lax.dot_general(a, b, (((1,), (1,)), ((), ())), preferred_element_type=F32)


def dot_tn(a, b):
    return lax.dot_general(a, b, (((0,), (0,)), ((), ())), preferred_element_type=F32)


def kernel(
    norm_factor,
    tok_ref,
    cot_ref,
    gain_ref,
    bias_ref,
    wqkv_hbm,
    wout_hbm,
    y_ref,
    tg_ref,
    dqkv_ref,
    dout_ref,
    vec_ref,
    wqkv,
    wout,
    xin,
    cin,
    xhat_s,
    normed_t,
    cot_t,
    proj,
    gatt,
    att,
    grads,
    part,
    core_in,
    core_sum,
    xy_in,
    z_out,
    z_in,
    vec_s,
    vec_core,
    vec_xy,
    vec_z,
    ysend,
    tsend,
    local_sem,
    ex_send,
    ex_recv,
    core_send,
    core_recv,
    xy_send,
    xy_recv,
    z_send,
    z_recv,
):
    lat = lax.axis_index("lat")
    lon = lax.axis_index("lon")
    x_lo = lat // 8
    y = lax.rem(lat // 2, 4)
    core = lax.rem(lat, 2)
    x_hi = lon // 8
    z = lax.rem(lon, 8)
    x = x_hi * 2 + x_lo
    odd = core

    def wrap(v):
        return lax.rem(v + 16, 16)

    sibling = (lat + 1 - 2 * core, lon)
    plane = []
    for sx in range(NX):
        for sy in range(NY):
            if sx or sy:
                px = lax.rem(x + sx, NX)
                py = lax.rem(y + sy, NY)
                row = lax.rem(px, 2) * 4 + py
                plane.append(((row * 2 + core, (px // 2) * 8 + z), row, px // 2))
    column = []
    for s in range(1, NZ):
        pz = lax.rem(z + s, NZ)
        column.append(((lat, x_hi * 8 + pz), pz))

    send_to = [
        ((lat, wrap(lon + 1 - 2 * odd)), 0, 1 - odd, 2 + odd),
        ((wrap(lat + 1), wrap(lon - 1 + odd)), 1, 0, 1),
        ((wrap(lat + 1), wrap(lon + odd)), 1, 1, 0),
    ]
    give_back = [
        ((lat, wrap(lon - 1 + 2 * odd)), 0, 1 - odd, 2 + odd),
        ((wrap(lat - 1), wrap(lon + odd)), 1, 0, 1),
        ((wrap(lat - 1), wrap(lon - 1 + odd)), 1, 1, 0),
    ]

    load_wqkv = pltpu.make_async_copy(wqkv_hbm, wqkv, local_sem.at[0])
    load_wout = pltpu.make_async_copy(wout_hbm, wout, local_sem.at[1])

    barrier = pltpu.get_barrier_semaphore()
    friends = (
        [p[0] for p in send_to]
        + [p[0] for p in give_back]
        + [sibling]
        + [p[0] for p in plane]
        + [p[0] for p in column]
    )
    for peer in friends:
        pl.semaphore_signal(barrier, inc=1, device_id=peer, device_id_type=MESH)

    def quarter(ref, row_half, col_half):
        return ref.at[pl.ds(3 * row_half, 3), pl.ds(6 * col_half, 6)]

    own_x = pltpu.make_async_copy(quarter(tok_ref, 0, odd), xin.at[3 - odd], local_sem.at[2])
    own_c = pltpu.make_async_copy(quarter(cot_ref, 0, odd), cin.at[3 - odd], local_sem.at[3])
    own_x.start()
    load_wqkv.start()
    own_c.start()
    load_wout.start()
    pl.semaphore_wait(barrier, len(friends))

    enter = []
    for kind, (src, dst) in enumerate(((tok_ref, xin), (cot_ref, cin))):
        row = []
        for m, (peer, rh, ch, slot) in enumerate(send_to):
            copy = pltpu.make_async_remote_copy(
                src_ref=quarter(src, rh, ch),
                dst_ref=dst.at[slot],
                send_sem=ex_send.at[kind, m],
                recv_sem=ex_recv.at[kind, m],
                device_id=peer,
                device_id_type=MESH,
            )
            copy.start()
            row.append(copy)
        enter.append(row)

    own_x.wait()
    for copy in enter[0]:
        copy.wait_recv()
    tokens = xin[...].reshape(TOK, D).astype(F32)
    centered = tokens - jnp.mean(tokens, axis=-1, keepdims=True)
    inverse = lax.rsqrt(jnp.mean(centered * centered, axis=-1, keepdims=True) + 1e-05)
    xhat = centered * inverse
    xhat_s[...] = xhat
    normed = (xhat * gain_ref[...] + bias_ref[...]).astype(BF)
    load_wqkv.wait()
    proj[...] = dot(normed, wqkv[...]).astype(BF)
    normed_t[...] = normed.T
    own_c.wait()
    for copy in enter[1]:
        copy.wait_recv()
    load_wout.wait()
    cot = cin[...].reshape(TOK, D)
    gatt[...] = dot_nt(cot, wout[...]).astype(BF)
    cot_t[...] = cot.T

    slot_q = lax.broadcasted_iota(jnp.int32, (TOK, TOK), 0) // QUARTER
    slot_k = lax.broadcasted_iota(jnp.int32, (TOK, TOK), 1) // QUARTER
    lat_edge = (lat == 0).astype(jnp.int32)
    lon_edge = (lon == odd * (LON - 1)).astype(jnp.int32)
    apart = lat_edge * jnp.abs(slot_q // 2 - slot_k // 2) + lon_edge * jnp.abs(
        lax.rem(slot_q, 2) - lax.rem(slot_k, 2)
    )
    valid = apart == 0
    lane = lax.broadcasted_iota(jnp.int32, (TOK, 128), 1)
    low = lane < 64
    halves = (low.astype(F32).astype(BF), (1.0 - low.astype(F32)).astype(BF))
    probs = []
    for pair in range(4):
        at = slice(pair * 128, pair * 128 + 128)
        q2 = proj[:, at]
        k2 = proj[:, 512 + pair * 128 : 640 + pair * 128]
        v2 = proj[:, 1024 + pair * 128 : 1152 + pair * 128]
        g2 = gatt[:, at]
        mixed = []
        grad_v = []
        grad_q = []
        grad_k = []
        for half in halves:
            kh = k2 * half
            vh = v2 * half
            scores = jnp.where(valid, dot_nt(q2, kh) * 0.125, -1e30)
            top = jnp.max(scores, axis=-1, keepdims=True)
            e = jnp.exp(scores - top)
            p = e * (1.0 / jnp.sum(e, axis=-1, keepdims=True))
            p_low = p.astype(BF)
            mixed.append(dot(p_low, vh))
            grad_v.append(dot_tn(p_low, g2))
            gp = dot_nt(g2, vh)
            inner = jnp.sum(p * gp, axis=-1, keepdims=True)
            gs = (p * (gp - inner)).astype(BF)
            grad_q.append(dot(gs, kh))
            grad_k.append(dot_tn(gs, q2))
        att[:, at] = (mixed[0] + mixed[1]).astype(BF)
        grads[:, at] = ((grad_q[0] + grad_q[1]) * 0.125).astype(BF)
        grads[:, 512 + pair * 128 : 640 + pair * 128] = (
            jnp.where(low, grad_k[0], grad_k[1]) * 0.125
        ).astype(BF)
        grads[:, 1024 + pair * 128 : 1152 + pair * 128] = jnp.where(
            low, grad_v[0], grad_v[1]
        ).astype(BF)

    def store_part(phase, col, left, right):
        for block in range(4):
            rows = dot(left[block * 256 : block * 256 + 256, :], right).astype(BF)
            rows = rows.reshape(2, 2, 2, 32, 512)
            for t in range(2):
                for c in range(2):
                    part[phase, c, block * 2 + t, :, :, col : col + 512] = rows[t, c]

    def start_core(phase):
        copy = pltpu.make_async_remote_copy(
            src_ref=part.at[phase, 1 - core],
            dst_ref=core_in.at[phase],
            send_sem=core_send.at[phase],
            recv_sem=core_recv.at[phase],
            device_id=sibling,
            device_id_type=MESH,
        )
        copy.start()
        return copy

    def start_plane(phase):
        copies = []
        for n, (peer, row, hi) in enumerate(plane):
            copy = pltpu.make_async_remote_copy(
                src_ref=core_sum.at[phase, row, hi],
                dst_ref=xy_in.at[phase, n],
                send_sem=xy_send.at[phase, n],
                recv_sem=xy_recv.at[phase, n],
                device_id=peer,
                device_id_type=MESH,
            )
            copy.start()
            copies.append(copy)
        return copies

    def start_column(phase):
        copies = []
        for n, (peer, pz) in enumerate(column):
            copy = pltpu.make_async_remote_copy(
                src_ref=z_out.at[phase, pz],
                dst_ref=z_in.at[phase, n],
                send_sem=z_send.at[phase, n],
                recv_sem=z_recv.at[phase, n],
                device_id=peer,
                device_id_type=MESH,
            )
            copy.start()
            copies.append(copy)
        return copies

    def add_core(phase, copy):
        copy.wait_recv()
        for row in range(8):
            core_sum[phase, row] = (
                part[phase, core, row].astype(F32) + core_in[phase, row].astype(F32)
            ).astype(BF)

    store_part(0, 0, cot_t, att[...])
    store_part(0, 512, normed_t, grads[:, 1024:1536])
    core_0 = start_core(0)
    store_part(1, 0, normed_t, grads[:, 0:512])
    store_part(1, 512, normed_t, grads[:, 512:1024])
    core_1 = start_core(1)
    add_core(0, core_0)
    plane_0 = start_plane(0)
    gn = dot_nt(grads[...], wqkv[...])
    xh = xhat_s[...]
    vec_s[0:1, :] = jnp.sum(gn * xh, axis=0, keepdims=True)
    vec_s[1:2, :] = jnp.sum(gn, axis=0, keepdims=True)
    vec_1 = pltpu.make_async_remote_copy(
        src_ref=vec_s,
        dst_ref=vec_core,
        send_sem=core_send.at[2],
        recv_sem=core_recv.at[2],
        device_id=sibling,
        device_id_type=MESH,
    )
    vec_1.start()
    add_core(1, core_1)
    plane_1 = start_plane(1)

    gh = gn * gain_ref[...]
    first = jnp.mean(gh, axis=-1, keepdims=True)
    second = jnp.mean(gh * xh, axis=-1, keepdims=True)
    cot_wide = cin[...].reshape(TOK, D).astype(F32)
    tg = (cot_wide + (gh - first - xh * second) * inverse).astype(BF)
    tsend[...] = tg.reshape(4, 3, 6, 2, D)

    def start_back(kind, src, dst):
        copies = []
        for m, (peer, rh, ch, slot) in enumerate(give_back):
            copy = pltpu.make_async_remote_copy(
                src_ref=src.at[slot],
                dst_ref=quarter(dst, rh, ch),
                send_sem=ex_send.at[kind, m],
                recv_sem=ex_recv.at[kind, m],
                device_id=peer,
                device_id_type=MESH,
            )
            copy.start()
            copies.append(copy)
        own = pltpu.make_async_copy(src.at[3 - odd], quarter(dst, 0, odd), local_sem.at[2 + kind])
        own.start()
        return copies, own

    back_t, own_t = start_back(2, tsend, tg_ref)
    vec_1.wait_recv()
    vec_core[...] = vec_core[...] + vec_s[...]
    vec_2 = []
    for n, (peer, _, _) in enumerate(plane):
        copy = pltpu.make_async_remote_copy(
            src_ref=vec_core,
            dst_ref=vec_xy.at[n],
            send_sem=xy_send.at[2, n],
            recv_sem=xy_recv.at[2, n],
            device_id=peer,
            device_id_type=MESH,
        )
        copy.start()
        vec_2.append(copy)
    mixed_out = dot(att[...], wout[...])
    y_out = (xin[...].reshape(TOK, D).astype(F32) + mixed_out).astype(BF)
    ysend[...] = y_out.reshape(4, 3, 6, 2, D)
    back_y, own_y = start_back(3, ysend, y_ref)

    def add_plane(phase, copies):
        for copy in copies:
            copy.wait_recv()
        total = core_sum[phase, x_lo * 4 + y, x_hi].astype(F32)
        for n in range(len(copies)):
            total = total + xy_in[phase, n].astype(F32)
        z_out[phase] = total.astype(BF).reshape(8, 4, WIDTH)

    add_plane(0, plane_0)
    column_0 = start_column(0)
    for copy in vec_2:
        copy.wait_recv()
    vec_total = vec_core[...]
    for n in range(len(vec_2)):
        vec_total = vec_total + vec_xy[n]
    vec_s2 = vec_total
    vec_1.wait_send()
    vec_s[...] = vec_s2
    vec_3 = []
    for n, (peer, _) in enumerate(column):
        copy = pltpu.make_async_remote_copy(
            src_ref=vec_s,
            dst_ref=vec_z.at[n],
            send_sem=z_send.at[2, n],
            recv_sem=z_recv.at[2, n],
            device_id=peer,
            device_id_type=MESH,
        )
        copy.start()
        vec_3.append(copy)
    add_plane(1, plane_1)
    column_1 = start_column(1)

    def add_column(phase, copies):
        for copy in copies:
            copy.wait_recv()
        total = z_out[phase, z].astype(F32)
        for n in range(len(copies)):
            total = total + z_in[phase, n].astype(F32)
        return total * norm_factor

    done = add_column(0, column_0)
    dout_ref[...] = done[:, 0:512]
    dqkv_ref[:, 1024:1536] = done[:, 512:1024]
    for copy in vec_3:
        copy.wait_recv()
    vec_total = vec_s[...]
    for n in range(len(vec_3)):
        vec_total = vec_total + vec_z[n]
    place = lat * LON + lon
    for copy in vec_2:
        copy.wait_send()
    vec_core[...] = vec_total * norm_factor
    lanes = vec_core[:, pl.ds(pl.multiple_of((place // 32) * 128, 128), 128)]
    vec_ref[...] = pltpu.roll(lanes, 128 - 4 * lax.rem(place, 32), 1)
    done = add_column(1, column_1)
    dqkv_ref[:, 0:1024] = done
    for copy in back_t + back_y:
        copy.wait()
    own_t.wait()
    own_y.wait()
    for copy in enter[0] + enter[1] + plane_0 + plane_1 + column_0 + column_1 + vec_3:
        copy.wait_send()
    core_0.wait_send()
    core_1.wait_send()


def on_device(tokens, layer_norm_gain, layer_norm_bias, w_qkv, w_out, output_cotangent):
    total_tokens = tokens.shape[0] * tokens.shape[1] * tokens.shape[2] * LAT * LON
    norm_factor = 1.0 / math.sqrt(total_tokens)
    grid_shape = (6, 12, 2, D)
    anywhere = pl.BlockSpec(memory_space=pl.ANY)
    vmem = pl.BlockSpec(memory_space=pltpu.VMEM)
    dma = pltpu.SemaphoreType.DMA

    def body(*refs):
        kernel(norm_factor, *refs)

    y_out, token_gradient, d_qkv, d_out, vec = pl.pallas_call(
        body,
        out_shape=(
            jax.ShapeDtypeStruct(grid_shape, BF),
            jax.ShapeDtypeStruct(grid_shape, BF),
            jax.ShapeDtypeStruct((4, 1536), F32),
            jax.ShapeDtypeStruct((4, HD), F32),
            jax.ShapeDtypeStruct((2, 128), F32),
        ),
        in_specs=[anywhere, anywhere, vmem, vmem, anywhere, anywhere],
        out_specs=(anywhere, anywhere, vmem, vmem, vmem),
        scratch_shapes=[
            pltpu.VMEM((D, 1536), BF),
            pltpu.VMEM((HD, D), BF),
            pltpu.VMEM((4, 3, 6, 2, D), BF),
            pltpu.VMEM((4, 3, 6, 2, D), BF),
            pltpu.VMEM((TOK, D), F32),
            pltpu.VMEM((D, TOK), BF),
            pltpu.VMEM((D, TOK), BF),
            pltpu.VMEM((TOK, 1536), BF),
            pltpu.VMEM((TOK, HD), BF),
            pltpu.VMEM((TOK, HD), BF),
            pltpu.VMEM((TOK, 1536), BF),
            pltpu.VMEM((PHASES, 2, 8, 2, 32, WIDTH), BF),
            pltpu.VMEM((PHASES, 8, 2, 32, WIDTH), BF),
            pltpu.VMEM((PHASES, 8, 2, 32, WIDTH), BF),
            pltpu.VMEM((PHASES, 15, 32, WIDTH), BF),
            pltpu.VMEM((PHASES, 8, 4, WIDTH), BF),
            pltpu.VMEM((PHASES, 7, 4, WIDTH), BF),
            pltpu.VMEM((2, D), F32),
            pltpu.VMEM((2, D), F32),
            pltpu.VMEM((15, 2, D), F32),
            pltpu.VMEM((7, 2, D), F32),
            pltpu.VMEM((4, 3, 6, 2, D), BF),
            pltpu.VMEM((4, 3, 6, 2, D), BF),
            dma((6,)),
            dma((4, 3)),
            dma((4, 3)),
            dma((3,)),
            dma((3,)),
            dma((3, 15)),
            dma((3, 15)),
            dma((3, 7)),
            dma((3, 7)),
        ],
        compiler_params=pltpu.CompilerParams(
            collective_id=0, has_side_effects=True, vmem_limit_bytes=56 << 20
        ),
        name="window_step",
    )(
        tokens.transpose(1, 2, 0, 3),
        output_cotangent.transpose(1, 2, 0, 3),
        layer_norm_gain.reshape(1, D),
        layer_norm_bias.reshape(1, D),
        w_qkv,
        w_out,
    )
    return (
        y_out.transpose(2, 0, 1, 3),
        token_gradient.transpose(2, 0, 1, 3),
        d_qkv,
        d_out.T,
        vec[0, 0:4],
        vec[1, 0:4],
    )


def solution(mesh):
    in_specs = (P(None, "lat", "lon", None), P(), P(), P(), P(), P(None, "lat", "lon", None))
    out_specs = (
        P(None, "lat", "lon", None),
        P(None, "lat", "lon", None),
        P(("lat", "lon"), None),
        P(None, ("lat", "lon")),
        P(("lat", "lon")),
        P(("lat", "lon")),
    )
    return jax.shard_map(
        on_device, mesh=mesh, in_specs=in_specs, out_specs=out_specs, check_vma=False
    )
```

```python
import math

import jax
import jax.numpy as jnp
from jax import lax
from jax.experimental import pallas as pl
from jax.experimental.pallas import tpu as pltpu
from jax.sharding import PartitionSpec as P

MESH = pl.DeviceIdType.MESH
BF = jnp.bfloat16
F32 = jnp.float32

D = 1024
HD = 512
TOK = 144
QUARTER = 36
NX, NY, NZ = 4, 4, 8
LAT, LON = 16, 16


def dot(a, b):
    return jnp.dot(a, b, preferred_element_type=F32)


def dot_nt(a, b):
    return lax.dot_general(a, b, (((1,), (1,)), ((), ())), preferred_element_type=F32)


def dot_tn(a, b):
    return lax.dot_general(a, b, (((0,), (0,)), ((), ())), preferred_element_type=F32)


OUT, VAL, QUE, KEY = range(4)
X_FIRST = (OUT, QUE)


def kernel(
    norm_factor,
    tok_ref,
    cot_ref,
    gain_ref,
    bias_ref,
    wqkv_hbm,
    wout_hbm,
    y_ref,
    tg_ref,
    dqkv_ref,
    dout_ref,
    vec_ref,
    wqkv,
    wout,
    xin,
    cin,
    xhat_s,
    left,
    left_in,
    proj,
    gatt,
    probs,
    right,
    right_in,
    part,
    one_in,
    mid,
    two_in,
    z_out,
    z_in,
    vec_out,
    vec_core,
    vec_xy,
    vec_z,
    ysend,
    tsend,
    local_sem,
    ex_send,
    ex_recv,
    core_send,
    core_recv,
    one_send,
    one_recv,
    two_send,
    two_recv,
    z_send,
    z_recv,
    vec_send,
    vec_recv,
):
    lat = lax.axis_index("lat")
    lon = lax.axis_index("lon")
    x_lo = lat // 8
    y = lax.rem(lat // 2, 4)
    core = lax.rem(lat, 2)
    x_hi = lon // 8
    z = lax.rem(lon, 8)
    x = x_hi * 2 + x_lo
    odd = core

    def wrap(v):
        return lax.rem(v + 16, 16)

    sibling = (lat + 1 - 2 * core, lon)
    along_x = []
    for s in range(1, NX):
        px = lax.rem(x + s, NX)
        along_x.append(((lax.rem(px, 2) * 8 + y * 2 + core, (px // 2) * 8 + z), px))
    along_y = []
    for s in range(1, NY):
        py = lax.rem(y + s, NY)
        along_y.append((((x_lo * 4 + py) * 2 + core, lon), py))
    along_z = []
    for s in range(1, NZ):
        pz = lax.rem(z + s, NZ)
        along_z.append(((lat, x_hi * 8 + pz), pz))

    send_to = [
        ((lat, wrap(lon + 1 - 2 * odd)), 0, 1 - odd, 2 + odd),
        ((wrap(lat + 1), wrap(lon - 1 + odd)), 1, 0, 1),
        ((wrap(lat + 1), wrap(lon + odd)), 1, 1, 0),
    ]
    give_back = [
        ((lat, wrap(lon - 1 + 2 * odd)), 0, 1 - odd, 2 + odd),
        ((wrap(lat - 1), wrap(lon + odd)), 1, 0, 1),
        ((wrap(lat - 1), wrap(lon - 1 + odd)), 1, 1, 0),
    ]
    unsent = []

    def push(src, dst, send_sem, recv_sem, peer):
        copy = pltpu.make_async_remote_copy(
            src_ref=src,
            dst_ref=dst,
            send_sem=send_sem,
            recv_sem=recv_sem,
            device_id=peer,
            device_id_type=MESH,
        )
        copy.start()
        unsent.append(copy)
        return copy

    def arrived(copies):
        for copy in copies:
            copy.wait_recv()

    load_wqkv = pltpu.make_async_copy(wqkv_hbm, wqkv, local_sem.at[0])
    load_wout = pltpu.make_async_copy(wout_hbm, wout, local_sem.at[1])

    barrier = pltpu.get_barrier_semaphore()
    friends = [p[0] for p in along_z + along_x + along_y + send_to + give_back] + [sibling]
    for peer in friends:
        pl.semaphore_signal(barrier, inc=1, device_id=peer, device_id_type=MESH)

    def quarter(ref, row_half, col_half):
        return ref.at[pl.ds(3 * row_half, 3), pl.ds(6 * col_half, 6)]

    own_x = pltpu.make_async_copy(quarter(tok_ref, 0, odd), xin.at[3 - odd], local_sem.at[2])
    own_c = pltpu.make_async_copy(quarter(cot_ref, 0, odd), cin.at[3 - odd], local_sem.at[3])
    own_x.start()
    load_wqkv.start()
    own_c.start()
    load_wout.start()
    pl.semaphore_wait(barrier, len(friends))

    enter = []
    for kind, (src, dst) in enumerate(((tok_ref, xin), (cot_ref, cin))):
        enter.append(
            [
                push(
                    quarter(src, rh, ch),
                    dst.at[slot],
                    ex_send.at[kind, m],
                    ex_recv.at[kind, m],
                    peer,
                )
                for m, (peer, rh, ch, slot) in enumerate(send_to)
            ]
        )

    def share_left(kind, value):
        rows = value.reshape(8, 2, 64, TOK)
        for c in range(2):
            for t in range(8):
                left[kind, c, t] = rows[t, c]
        return push(
            left.at[kind, 1 - core],
            left_in.at[kind],
            core_send.at[kind],
            core_recv.at[kind],
            sibling,
        )

    own_x.wait()
    arrived(enter[0])
    tokens = xin[...].reshape(TOK, D).astype(F32)
    centered = tokens - jnp.mean(tokens, axis=-1, keepdims=True)
    inverse = lax.rsqrt(jnp.mean(centered * centered, axis=-1, keepdims=True) + 1e-05)
    xhat = centered * inverse
    xhat_s[...] = xhat
    normed = (xhat * gain_ref[...] + bias_ref[...]).astype(BF)
    load_wqkv.wait()
    proj[...] = dot(normed, wqkv[...]).astype(BF)
    left_n = share_left(0, normed.T)
    own_c.wait()
    arrived(enter[1])
    load_wout.wait()
    cot = cin[...].reshape(TOK, D)
    gatt[...] = dot_nt(cot, wout[...]).astype(BF)
    left_c = share_left(1, cot.T)

    slot_q = lax.broadcasted_iota(jnp.int32, (TOK, TOK), 0) // QUARTER
    slot_k = lax.broadcasted_iota(jnp.int32, (TOK, TOK), 1) // QUARTER
    lat_edge = (lat == 0).astype(jnp.int32)
    lon_edge = (lon == odd * (LON - 1)).astype(jnp.int32)
    apart = lat_edge * jnp.abs(slot_q // 2 - slot_k // 2) + lon_edge * jnp.abs(
        lax.rem(slot_q, 2) - lax.rem(slot_k, 2)
    )
    valid = apart == 0
    lane = lax.broadcasted_iota(jnp.int32, (TOK, 128), 1)
    low = lane < 64
    halves = (low.astype(F32).astype(BF), (1.0 - low.astype(F32)).astype(BF))

    def share_right(chunk):
        return push(
            right.at[chunk],
            right_in.at[chunk],
            core_send.at[2 + chunk],
            core_recv.at[2 + chunk],
            sibling,
        )

    for pair in range(4):
        at = slice(pair * 128, pair * 128 + 128)
        q2 = proj[:, at]
        k2 = proj[:, 512 + pair * 128 : 640 + pair * 128]
        v2 = proj[:, 1024 + pair * 128 : 1152 + pair * 128]
        g2 = gatt[:, at]
        mixed = []
        grad_v = []
        for h, half in enumerate(halves):
            scores = jnp.where(valid, dot_nt(q2, k2 * half) * 0.125, -1e30)
            top = jnp.max(scores, axis=-1, keepdims=True)
            e = jnp.exp(scores - top)
            p = e * (1.0 / jnp.sum(e, axis=-1, keepdims=True))
            probs[pair * 2 + h] = p
            p_low = p.astype(BF)
            mixed.append(dot(p_low, v2 * half))
            grad_v.append(dot_tn(p_low, g2))
        right[OUT, :, at] = (mixed[0] + mixed[1]).astype(BF)
        right[VAL, :, at] = jnp.where(low, grad_v[0], grad_v[1]).astype(BF)
    right_copies = [share_right(OUT), share_right(VAL)]
    for pair in range(4):
        at = slice(pair * 128, pair * 128 + 128)
        q2 = proj[:, at]
        k2 = proj[:, 512 + pair * 128 : 640 + pair * 128]
        v2 = proj[:, 1024 + pair * 128 : 1152 + pair * 128]
        g2 = gatt[:, at]
        grad_q = []
        grad_k = []
        for h, half in enumerate(halves):
            p = probs[pair * 2 + h]
            gp = dot_nt(g2, v2 * half)
            inner = jnp.sum(p * gp, axis=-1, keepdims=True)
            gs = (p * (gp - inner)).astype(BF)
            grad_q.append(dot(gs, k2 * half))
            grad_k.append(dot_tn(gs, q2))
        right[QUE, :, at] = ((grad_q[0] + grad_q[1]) * 0.125).astype(BF)
        right[KEY, :, at] = (jnp.where(low, grad_k[0], grad_k[1]) * 0.125).astype(BF)
    right_copies += [share_right(QUE), share_right(KEY)]

    def first_step(chunk):
        kind = 1 if chunk == OUT else 0
        x_first = chunk in X_FIRST
        right_copies[chunk].wait_recv()
        mine = right[chunk]
        other = right_in[chunk]
        for block in range(2):
            at = slice(block * 4, block * 4 + 4)
            rows = dot(left[kind, core, at].reshape(256, TOK), mine) + dot(
                left_in[kind, at].reshape(256, TOK), other
            )
            rows = rows.astype(BF).reshape(4, 2, 32, 512)
            for t in range(4):
                for hi in range(2):
                    gx = hi * 2 + block
                    if x_first:
                        part[chunk, gx, t] = rows[t, hi]
                    else:
                        part[chunk, t, gx] = rows[t, hi]
        return [
            push(
                part.at[chunk, place],
                one_in.at[chunk, n],
                one_send.at[chunk, n],
                one_recv.at[chunk, n],
                peer,
            )
            for n, (peer, place) in enumerate(along_x if x_first else along_y)
        ]

    def second_step(chunk, copies):
        x_first = chunk in X_FIRST
        arrived(copies)
        total = part[chunk, x if x_first else y].astype(F32)
        for n in range(3):
            total = total + one_in[chunk, n].astype(F32)
        mid[chunk] = total.astype(BF)
        return [
            push(
                mid.at[chunk, place],
                two_in.at[chunk, n],
                two_send.at[chunk, n],
                two_recv.at[chunk, n],
                peer,
            )
            for n, (peer, place) in enumerate(along_y if x_first else along_x)
        ]

    def third_step(phase, pair):
        for col, (chunk, copies) in enumerate(pair):
            arrived(copies)
            total = mid[chunk, y if chunk in X_FIRST else x].astype(F32)
            for n in range(3):
                total = total + two_in[chunk, n].astype(F32)
            z_out[phase, :, :, col * 512 : col * 512 + 512] = total.astype(BF).reshape(8, 4, 512)
        return [
            push(
                z_out.at[phase, place],
                z_in.at[phase, n],
                z_send.at[phase, n],
                z_recv.at[phase, n],
                peer,
            )
            for n, (peer, place) in enumerate(along_z)
        ]

    def last_step(phase, copies):
        arrived(copies)
        total = z_out[phase, z].astype(F32)
        for n in range(7):
            total = total + z_in[phase, n].astype(F32)
        return total * norm_factor

    def start_back(kind, src, dst):
        for m, (peer, rh, ch, slot) in enumerate(give_back):
            back.append(
                push(
                    src.at[slot],
                    quarter(dst, rh, ch),
                    ex_send.at[kind, m],
                    ex_recv.at[kind, m],
                    peer,
                )
            )
        own = pltpu.make_async_copy(src.at[3 - odd], quarter(dst, 0, odd), local_sem.at[2 + kind])
        own.start()
        return own

    back = []
    left_c.wait_recv()
    one_out = first_step(OUT)
    left_n.wait_recv()
    one_val = first_step(VAL)
    one_que = first_step(QUE)
    one_key = first_step(KEY)

    gn = dot_nt(right[QUE], wqkv[:, 0:512])
    gn = gn + dot_nt(right[KEY], wqkv[:, 512:1024])
    gn = gn + dot_nt(right[VAL], wqkv[:, 1024:1536])
    xh = xhat_s[...]
    vec_out[0, 0:1, :] = jnp.sum(gn * xh, axis=0, keepdims=True)
    vec_out[0, 1:2, :] = jnp.sum(gn, axis=0, keepdims=True)
    vec_0 = push(vec_out.at[0], vec_core, vec_send.at[0], vec_recv.at[0], sibling)
    gh = gn * gain_ref[...]
    first = jnp.mean(gh, axis=-1, keepdims=True)
    second = jnp.mean(gh * xh, axis=-1, keepdims=True)
    cot_wide = cin[...].reshape(TOK, D).astype(F32)
    tg = (cot_wide + (gh - first - xh * second) * inverse).astype(BF)
    tsend[...] = tg.reshape(4, 3, 6, 2, D)

    def vec_step(stage, total, peers, landing, first_sem):
        vec_out[stage] = total
        return [
            push(
                vec_out.at[stage],
                landing.at[n],
                vec_send.at[first_sem + n],
                vec_recv.at[first_sem + n],
                peer[0],
            )
            for n, peer in enumerate(peers)
        ]

    vec_0.wait_recv()
    vec_1 = vec_step(1, vec_out[0] + vec_core[...], along_x, vec_xy.at[0], 1)
    own_t = start_back(2, tsend, tg_ref)
    mixed_out = dot(right[OUT], wout[...])
    y_out = (xin[...].reshape(TOK, D).astype(F32) + mixed_out).astype(BF)
    ysend[...] = y_out.reshape(4, 3, 6, 2, D)
    own_y = start_back(3, ysend, y_ref)

    two_out = second_step(OUT, one_out)
    two_val = second_step(VAL, one_val)
    arrived(vec_1)
    total = vec_out[1]
    for n in range(3):
        total = total + vec_xy[0, n]
    vec_2 = vec_step(2, total, along_y, vec_xy.at[1], 4)
    two_que = second_step(QUE, one_que)
    two_key = second_step(KEY, one_key)
    z_first = third_step(0, ((OUT, two_out), (VAL, two_val)))
    arrived(vec_2)
    total = vec_out[2]
    for n in range(3):
        total = total + vec_xy[1, n]
    vec_3 = vec_step(3, total, along_z, vec_z, 7)
    z_second = third_step(1, ((QUE, two_que), (KEY, two_key)))

    done = last_step(0, z_first)
    dout_ref[...] = done[:, 0:512]
    dqkv_ref[:, 1024:1536] = done[:, 512:1024]
    arrived(vec_3)
    total = vec_out[3]
    for n in range(7):
        total = total + vec_z[n]
    place = lat * LON + lon
    vec_out[4] = total * norm_factor
    lanes = vec_out[4, :, pl.ds(pl.multiple_of((place // 32) * 128, 128), 128)]
    vec_ref[...] = pltpu.roll(lanes, 128 - 4 * lax.rem(place, 32), 1)
    done = last_step(1, z_second)
    dqkv_ref[:, 0:1024] = done
    arrived(back)
    own_t.wait()
    own_y.wait()
    for copy in unsent:
        copy.wait_send()


def finish(y_in, tg_in, dqkv_in, dout_in, vec_in, y_out, tg_out, dqkv_out, dout_out, gain_out, bias_out, sems):
    copies = [
        pltpu.make_async_copy(src, dst, sems.at[n])
        for n, (src, dst) in enumerate(
            ((y_in, y_out), (tg_in, tg_out), (dqkv_in, dqkv_out), (dout_in, dout_out))
        )
    ]
    for copy in copies:
        copy.start()
    gain_out[...] = vec_in[0:1, 0:4]
    bias_out[...] = vec_in[1:2, 0:4]
    for copy in copies:
        copy.wait()


def on_device(tokens, layer_norm_gain, layer_norm_bias, w_qkv, w_out, output_cotangent):
    total_tokens = tokens.shape[0] * tokens.shape[1] * tokens.shape[2] * LAT * LON
    norm_factor = 1.0 / math.sqrt(total_tokens)
    grid = jax.ShapeDtypeStruct((6, 12, 2, D), BF)
    d_qkv_shape = jax.ShapeDtypeStruct((4, 1536), F32)
    d_out_shape = jax.ShapeDtypeStruct((4, HD), F32)
    anywhere = pl.BlockSpec(memory_space=pl.ANY)
    vmem = pl.BlockSpec(memory_space=pltpu.VMEM)
    dma = pltpu.SemaphoreType.DMA

    def body(*refs):
        kernel(norm_factor, *refs)

    results = pl.pallas_call(
        body,
        out_shape=(
            pltpu.VMEM((6, 12, 2, D), BF),
            pltpu.VMEM((6, 12, 2, D), BF),
            pltpu.VMEM((4, 1536), F32),
            pltpu.VMEM((4, HD), F32),
            pltpu.VMEM((2, 128), F32),
        ),
        in_specs=[anywhere, anywhere, vmem, vmem, anywhere, anywhere],
        out_specs=(vmem,) * 5,
        scratch_shapes=[
            pltpu.VMEM((D, 1536), BF),
            pltpu.VMEM((HD, D), BF),
            pltpu.VMEM((4, 3, 6, 2, D), BF),
            pltpu.VMEM((4, 3, 6, 2, D), BF),
            pltpu.VMEM((TOK, D), F32),
            pltpu.VMEM((2, 2, 8, 64, TOK), BF),
            pltpu.VMEM((2, 8, 64, TOK), BF),
            pltpu.VMEM((TOK, 1536), BF),
            pltpu.VMEM((TOK, HD), BF),
            pltpu.VMEM((8, TOK, TOK), F32),
            pltpu.VMEM((4, TOK, HD), BF),
            pltpu.VMEM((4, TOK, HD), BF),
            pltpu.VMEM((4, 4, 4, 32, HD), BF),
            pltpu.VMEM((4, 3, 4, 32, HD), BF),
            pltpu.VMEM((4, 4, 32, HD), BF),
            pltpu.VMEM((4, 3, 32, HD), BF),
            pltpu.VMEM((2, 8, 4, 2 * HD), BF),
            pltpu.VMEM((2, 7, 4, 2 * HD), BF),
            pltpu.VMEM((5, 2, D), F32),
            pltpu.VMEM((2, D), F32),
            pltpu.VMEM((2, 3, 2, D), F32),
            pltpu.VMEM((7, 2, D), F32),
            pltpu.VMEM((4, 3, 6, 2, D), BF),
            pltpu.VMEM((4, 3, 6, 2, D), BF),
            dma((6,)),
            dma((4, 3)),
            dma((4, 3)),
            dma((6,)),
            dma((6,)),
            dma((4, 3)),
            dma((4, 3)),
            dma((4, 3)),
            dma((4, 3)),
            dma((2, 7)),
            dma((2, 7)),
            dma((14,)),
            dma((14,)),
        ],
        compiler_params=pltpu.CompilerParams(
            collective_id=0, has_side_effects=True, vmem_limit_bytes=56 << 20
        ),
        name="window_step",
    )(
        tokens.transpose(1, 2, 0, 3),
        output_cotangent.transpose(1, 2, 0, 3),
        layer_norm_gain.reshape(1, D),
        layer_norm_bias.reshape(1, D),
        w_qkv,
        w_out,
    )
    small = jax.ShapeDtypeStruct((1, 4), F32)
    y_out, token_gradient, d_qkv, d_out, gain_gradient, d_bias = pl.pallas_call(
        finish,
        out_shape=(grid, grid, d_qkv_shape, d_out_shape, small, small),
        in_specs=[vmem] * 5,
        out_specs=(anywhere, anywhere, anywhere, anywhere, vmem, vmem),
        scratch_shapes=[dma((4,))],
        name="hand_out",
    )(*[pltpu.with_memory_space_constraint(r, pltpu.VMEM) for r in results])
    return (
        y_out.transpose(2, 0, 1, 3),
        token_gradient.transpose(2, 0, 1, 3),
        d_qkv,
        d_out.T,
        gain_gradient.reshape(4),
        d_bias.reshape(4),
    )


def solution(mesh):
    in_specs = (P(None, "lat", "lon", None), P(), P(), P(), P(), P(None, "lat", "lon", None))
    out_specs = (
        P(None, "lat", "lon", None),
        P(None, "lat", "lon", None),
        P(("lat", "lon"), None),
        P(None, ("lat", "lon")),
        P(("lat", "lon")),
        P(("lat", "lon")),
    )
    return jax.shard_map(
        on_device, mesh=mesh, in_specs=in_specs, out_specs=out_specs, check_vma=False
    )
```

```python
import math

import jax
import jax.numpy as jnp
from jax import lax
from jax.experimental import pallas as pl
from jax.experimental.pallas import tpu as pltpu
from jax.sharding import PartitionSpec as P

MESH = pl.DeviceIdType.MESH
BF = jnp.bfloat16
F32 = jnp.float32

D = 1024
HD = 512
TOK = 144
QUARTER = 36
NX, NY, NZ = 4, 4, 8
LAT, LON = 16, 16


def dot(a, b):
    return jnp.dot(a, b, preferred_element_type=F32)


def dot_nt(a, b):
    return lax.dot_general(a, b, (((1,), (1,)), ((), ())), preferred_element_type=F32)


def dot_tn(a, b):
    return lax.dot_general(a, b, (((0,), (0,)), ((), ())), preferred_element_type=F32)


OUT, VAL, QUE, KEY = range(4)
X_FIRST = (OUT, QUE)


def kernel(
    norm_factor,
    tok_ref,
    cot_ref,
    gain_hbm,
    bias_hbm,
    wqkv_hbm,
    wout_hbm,
    y_ref,
    tg_ref,
    dqkv_ref,
    dout_ref,
    vec_ref,
    gain_ref,
    bias_ref,
    wqkv,
    wout,
    xin,
    cin,
    xhat_s,
    left,
    left_in,
    proj,
    gatt,
    probs,
    right,
    right_in,
    part,
    one_in,
    mid,
    two_in,
    z_out,
    z_in,
    vec_out,
    vec_core,
    vec_xy,
    vec_z,
    ysend,
    tsend,
    local_sem,
    ex_send,
    ex_recv,
    core_send,
    core_recv,
    one_send,
    one_recv,
    two_send,
    two_recv,
    z_send,
    z_recv,
    vec_send,
    vec_recv,
):
    lat = lax.axis_index("lat")
    lon = lax.axis_index("lon")
    x_lo = lat // 8
    y = lax.rem(lat // 2, 4)
    core = lax.rem(lat, 2)
    x_hi = lon // 8
    z = lax.rem(lon, 8)
    x = x_hi * 2 + x_lo
    odd = core

    def wrap(v):
        return lax.rem(v + 16, 16)

    sibling = (lat + 1 - 2 * core, lon)
    along_x = []
    for s in range(1, NX):
        px = lax.rem(x + s, NX)
        along_x.append(((lax.rem(px, 2) * 8 + y * 2 + core, (px // 2) * 8 + z), px))
    along_y = []
    for s in range(1, NY):
        py = lax.rem(y + s, NY)
        along_y.append((((x_lo * 4 + py) * 2 + core, lon), py))
    along_z = []
    for s in range(1, NZ):
        pz = lax.rem(z + s, NZ)
        along_z.append(((lat, x_hi * 8 + pz), pz))

    send_to = [
        ((lat, wrap(lon + 1 - 2 * odd)), 0, 1 - odd, 2 + odd),
        ((wrap(lat + 1), wrap(lon - 1 + odd)), 1, 0, 1),
        ((wrap(lat + 1), wrap(lon + odd)), 1, 1, 0),
    ]
    give_back = [
        ((lat, wrap(lon - 1 + 2 * odd)), 0, 1 - odd, 2 + odd),
        ((wrap(lat - 1), wrap(lon + odd)), 1, 0, 1),
        ((wrap(lat - 1), wrap(lon - 1 + odd)), 1, 1, 0),
    ]
    unsent = []

    def push(src, dst, send_sem, recv_sem, peer):
        copy = pltpu.make_async_remote_copy(
            src_ref=src,
            dst_ref=dst,
            send_sem=send_sem,
            recv_sem=recv_sem,
            device_id=peer,
            device_id_type=MESH,
        )
        copy.start()
        unsent.append(copy)
        return copy

    def arrived(copies):
        for copy in copies:
            copy.wait_recv()

    load_wqkv = pltpu.make_async_copy(wqkv_hbm, wqkv, local_sem.at[0])
    load_wout = pltpu.make_async_copy(wout_hbm, wout, local_sem.at[1])
    load_gain = pltpu.make_async_copy(gain_hbm, gain_ref, local_sem.at[6])
    load_bias = pltpu.make_async_copy(bias_hbm, bias_ref, local_sem.at[7])

    barrier = pltpu.get_barrier_semaphore()
    friends = [p[0] for p in send_to + give_back + along_z + along_x + along_y] + [sibling]
    for peer in friends:
        pl.semaphore_signal(barrier, inc=1, device_id=peer, device_id_type=MESH)

    def quarter(ref, row_half, col_half):
        return ref.at[pl.ds(3 * row_half, 3), pl.ds(6 * col_half, 6)]

    own_x = pltpu.make_async_copy(quarter(tok_ref, 0, odd), xin.at[3 - odd], local_sem.at[2])
    own_c = pltpu.make_async_copy(quarter(cot_ref, 0, odd), cin.at[3 - odd], local_sem.at[3])
    own_x.start()
    load_gain.start()
    load_bias.start()
    load_wqkv.start()
    own_c.start()
    load_wout.start()
    pl.semaphore_wait(barrier, len(friends))

    enter = []
    for kind, (src, dst) in enumerate(((tok_ref, xin), (cot_ref, cin))):
        enter.append(
            [
                push(
                    quarter(src, rh, ch),
                    dst.at[slot],
                    ex_send.at[kind, m],
                    ex_recv.at[kind, m],
                    peer,
                )
                for m, (peer, rh, ch, slot) in enumerate(send_to)
            ]
        )

    def share_left(kind, value):
        rows = value.reshape(8, 2, 64, TOK)
        for c in range(2):
            for t in range(8):
                left[kind, c, t] = rows[t, c]
        return push(
            left.at[kind, 1 - core],
            left_in.at[kind],
            core_send.at[kind],
            core_recv.at[kind],
            sibling,
        )

    own_x.wait()
    load_gain.wait()
    load_bias.wait()
    arrived(enter[0])
    tokens = xin[...].reshape(TOK, D).astype(F32)
    centered = tokens - jnp.mean(tokens, axis=-1, keepdims=True)
    inverse = lax.rsqrt(jnp.mean(centered * centered, axis=-1, keepdims=True) + 1e-05)
    xhat = centered * inverse
    xhat_s[...] = xhat
    normed = (xhat * gain_ref[...] + bias_ref[...]).astype(BF)
    load_wqkv.wait()
    proj[...] = dot(normed, wqkv[...]).astype(BF)

    slot_q = lax.broadcasted_iota(jnp.int32, (TOK, TOK), 0) // QUARTER
    slot_k = lax.broadcasted_iota(jnp.int32, (TOK, TOK), 1) // QUARTER
    lat_edge = (lat == 0).astype(jnp.int32)
    lon_edge = (lon == odd * (LON - 1)).astype(jnp.int32)
    apart = lat_edge * jnp.abs(slot_q // 2 - slot_k // 2) + lon_edge * jnp.abs(
        lax.rem(slot_q, 2) - lax.rem(slot_k, 2)
    )
    valid = apart == 0
    lane = lax.broadcasted_iota(jnp.int32, (TOK, 128), 1)
    low = lane < 64
    halves = (low.astype(F32).astype(BF), (1.0 - low.astype(F32)).astype(BF))

    def share_right(chunk):
        return push(
            right.at[chunk],
            right_in.at[chunk],
            core_send.at[2 + chunk],
            core_recv.at[2 + chunk],
            sibling,
        )

    def columns(pair):
        at = slice(pair * 128, pair * 128 + 128)
        q2 = proj[:, at]
        k2 = proj[:, 512 + pair * 128 : 640 + pair * 128]
        v2 = proj[:, 1024 + pair * 128 : 1152 + pair * 128]
        return at, q2, k2, v2

    def forward(pair):
        at, q2, k2, v2 = columns(pair)
        mixed = []
        for h, half in enumerate(halves):
            scores = jnp.where(valid, dot_nt(k2 * half, q2) * 0.125, -1e30)
            top = jnp.max(scores, axis=0, keepdims=True)
            e = jnp.exp(scores - top)
            p = e * (1.0 / jnp.sum(e, axis=0, keepdims=True))
            probs[pair * 2 + h] = p
            mixed.append(dot_tn(p.astype(BF), v2 * half))
        right[OUT, :, at] = (mixed[0] + mixed[1]).astype(BF)

    def value_gradient(pair):
        at = slice(pair * 128, pair * 128 + 128)
        g2 = gatt[:, at]
        grad_v = [dot(probs[pair * 2 + h].astype(BF), g2) for h in range(2)]
        right[VAL, :, at] = jnp.where(low, grad_v[0], grad_v[1]).astype(BF)

    def backward(pair):
        at, q2, k2, v2 = columns(pair)
        g2 = gatt[:, at]
        grad_q = []
        grad_k = []
        for h, half in enumerate(halves):
            p = probs[pair * 2 + h]
            gp = dot_nt(v2 * half, g2)
            inner = jnp.sum(p * gp, axis=0, keepdims=True)
            gs = (p * (gp - inner)).astype(BF)
            grad_q.append(dot_tn(gs, k2 * half))
            grad_k.append(dot(gs, q2))
        right[QUE, :, at] = ((grad_q[0] + grad_q[1]) * 0.125).astype(BF)
        right[KEY, :, at] = (jnp.where(low, grad_k[0], grad_k[1]) * 0.125).astype(BF)

    def first_step(chunk):
        kind = 1 if chunk == OUT else 0
        x_first = chunk in X_FIRST
        right_copies[chunk].wait_recv()
        mine = right[chunk]
        other = right_in[chunk]
        for block in range(2):
            at = slice(block * 4, block * 4 + 4)
            rows = dot(left[kind, core, at].reshape(256, TOK), mine) + dot(
                left_in[kind, at].reshape(256, TOK), other
            )
            rows = rows.astype(BF).reshape(4, 2, 32, 512)
            for t in range(4):
                for hi in range(2):
                    gx = hi * 2 + block
                    if x_first:
                        part[chunk, gx, t] = rows[t, hi]
                    else:
                        part[chunk, t, gx] = rows[t, hi]
        return [
            push(
                part.at[chunk, place],
                one_in.at[chunk, n],
                one_send.at[chunk, n],
                one_recv.at[chunk, n],
                peer,
            )
            for n, (peer, place) in enumerate(along_x if x_first else along_y)
        ]

    def second_step(chunk, copies):
        x_first = chunk in X_FIRST
        arrived(copies)
        total = part[chunk, x if x_first else y].astype(F32)
        for n in range(3):
            total = total + one_in[chunk, n].astype(F32)
        mid[chunk] = total.astype(BF)
        return [
            push(
                mid.at[chunk, place],
                two_in.at[chunk, n],
                two_send.at[chunk, n],
                two_recv.at[chunk, n],
                peer,
            )
            for n, (peer, place) in enumerate(along_y if x_first else along_x)
        ]

    def third_step(phase, pair):
        for col, (chunk, copies) in enumerate(pair):
            arrived(copies)
            total = mid[chunk, y if chunk in X_FIRST else x].astype(F32)
            for n in range(3):
                total = total + two_in[chunk, n].astype(F32)
            z_out[phase, :, :, col * 512 : col * 512 + 512] = total.astype(BF).reshape(8, 4, 512)
        return [
            push(
                z_out.at[phase, place],
                z_in.at[phase, n],
                z_send.at[phase, n],
                z_recv.at[phase, n],
                peer,
            )
            for n, (peer, place) in enumerate(along_z)
        ]

    def last_step(phase, copies):
        arrived(copies)
        total = z_out[phase, z].astype(F32)
        for n in range(7):
            total = total + z_in[phase, n].astype(F32)
        return total * norm_factor

    def start_back(kind, src, dst):
        for m, (peer, rh, ch, slot) in enumerate(give_back):
            back.append(
                push(
                    src.at[slot],
                    quarter(dst, rh, ch),
                    ex_send.at[kind, m],
                    ex_recv.at[kind, m],
                    peer,
                )
            )
        own = pltpu.make_async_copy(src.at[3 - odd], quarter(dst, 0, odd), local_sem.at[2 + kind])
        own.start()
        return own

    back = []
    for pair in range(4):
        forward(pair)
    right_copies = [share_right(OUT)]
    own_c.wait()
    arrived(enter[1])
    load_wout.wait()
    cot = cin[...].reshape(TOK, D)
    left_c = share_left(1, cot.T)
    gatt[...] = dot_nt(cot, wout[...]).astype(BF)
    for pair in range(4):
        value_gradient(pair)
    right_copies.append(share_right(VAL))
    left_n = share_left(0, normed.T)
    mixed_out = dot(right[OUT], wout[...])
    y_out = (xin[...].reshape(TOK, D).astype(F32) + mixed_out).astype(BF)
    ysend[...] = y_out.reshape(4, 3, 6, 2, D)
    own_y = start_back(3, ysend, y_ref)
    left_c.wait_recv()
    one_out = first_step(OUT)
    left_n.wait_recv()
    one_val = first_step(VAL)
    backward(0)
    backward(1)
    backward(2)
    backward(3)
    right_copies += [share_right(QUE), share_right(KEY)]

    gn = dot_nt(right[QUE], wqkv[:, 0:512])
    gn = gn + dot_nt(right[KEY], wqkv[:, 512:1024])
    gn = gn + dot_nt(right[VAL], wqkv[:, 1024:1536])
    xh = xhat_s[...]
    vec_out[0, 0:1, :] = jnp.sum(gn * xh, axis=0, keepdims=True)
    vec_out[0, 1:2, :] = jnp.sum(gn, axis=0, keepdims=True)
    vec_0 = push(vec_out.at[0], vec_core, vec_send.at[0], vec_recv.at[0], sibling)
    one_que = first_step(QUE)
    one_key = first_step(KEY)
    gh = gn * gain_ref[...]
    first = jnp.mean(gh, axis=-1, keepdims=True)
    second = jnp.mean(gh * xh, axis=-1, keepdims=True)
    cot_wide = cin[...].reshape(TOK, D).astype(F32)
    tg = (cot_wide + (gh - first - xh * second) * inverse).astype(BF)
    tsend[...] = tg.reshape(4, 3, 6, 2, D)

    def vec_step(stage, total, peers, landing, first_sem):
        vec_out[stage] = total
        return [
            push(
                vec_out.at[stage],
                landing.at[n],
                vec_send.at[first_sem + n],
                vec_recv.at[first_sem + n],
                peer[0],
            )
            for n, peer in enumerate(peers)
        ]

    vec_0.wait_recv()
    vec_1 = vec_step(1, vec_out[0] + vec_core[...], along_x, vec_xy.at[0], 1)

    two_out = second_step(OUT, one_out)
    two_val = second_step(VAL, one_val)
    arrived(vec_1)
    total = vec_out[1]
    for n in range(3):
        total = total + vec_xy[0, n]
    vec_2 = vec_step(2, total, along_y, vec_xy.at[1], 4)
    two_que = second_step(QUE, one_que)
    two_key = second_step(KEY, one_key)
    own_t = start_back(2, tsend, tg_ref)
    z_first = third_step(0, ((OUT, two_out), (VAL, two_val)))
    arrived(vec_2)
    total = vec_out[2]
    for n in range(3):
        total = total + vec_xy[1, n]
    vec_3 = vec_step(3, total, along_z, vec_z, 7)
    z_second = third_step(1, ((QUE, two_que), (KEY, two_key)))

    last_sends = z_second + vec_3
    for copy in unsent[: len(unsent) - len(last_sends)]:
        copy.wait_send()
    arrived(back)
    own_t.wait()
    own_y.wait()
    done = last_step(0, z_first)
    dout_ref[...] = done[:, 0:512]
    dqkv_ref[:, 1024:1536] = done[:, 512:1024]
    arrived(vec_3)
    total = vec_out[3]
    for n in range(7):
        total = total + vec_z[n]
    place = lat * LON + lon
    vec_out[4] = total * norm_factor
    lanes = vec_out[4, :, pl.ds(pl.multiple_of((place // 32) * 128, 128), 128)]
    vec_ref[...] = pltpu.roll(lanes, 128 - 4 * lax.rem(place, 32), 1)
    done = last_step(1, z_second)
    dqkv_ref[:, 0:1024] = done
    for copy in last_sends:
        copy.wait_send()


def finish(y_in, tg_in, dqkv_in, dout_in, vec_in, y_out, tg_out, dqkv_out, dout_out, gain_out, bias_out, sems):
    copies = [
        pltpu.make_async_copy(src, dst, sems.at[n])
        for n, (src, dst) in enumerate(
            ((y_in, y_out), (tg_in, tg_out), (dqkv_in, dqkv_out), (dout_in, dout_out))
        )
    ]
    for copy in copies:
        copy.start()
    gain_out[...] = vec_in[0:1, 0:4]
    bias_out[...] = vec_in[1:2, 0:4]
    for copy in copies:
        copy.wait()


def on_device(tokens, layer_norm_gain, layer_norm_bias, w_qkv, w_out, output_cotangent):
    total_tokens = tokens.shape[0] * tokens.shape[1] * tokens.shape[2] * LAT * LON
    norm_factor = 1.0 / math.sqrt(total_tokens)
    grid = jax.ShapeDtypeStruct((6, 12, 2, D), BF)
    d_qkv_shape = jax.ShapeDtypeStruct((4, 1536), F32)
    d_out_shape = jax.ShapeDtypeStruct((4, HD), F32)
    anywhere = pl.BlockSpec(memory_space=pl.ANY)
    vmem = pl.BlockSpec(memory_space=pltpu.VMEM)
    dma = pltpu.SemaphoreType.DMA

    def body(*refs):
        kernel(norm_factor, *refs)

    results = pl.pallas_call(
        body,
        out_shape=(
            pltpu.VMEM((6, 12, 2, D), BF),
            pltpu.VMEM((6, 12, 2, D), BF),
            pltpu.VMEM((4, 1536), F32),
            pltpu.VMEM((4, HD), F32),
            pltpu.VMEM((2, 128), F32),
        ),
        in_specs=[anywhere] * 6,
        out_specs=(vmem,) * 5,
        scratch_shapes=[
            pltpu.VMEM((1, D), F32),
            pltpu.VMEM((1, D), F32),
            pltpu.VMEM((D, 1536), BF),
            pltpu.VMEM((HD, D), BF),
            pltpu.VMEM((4, 3, 6, 2, D), BF),
            pltpu.VMEM((4, 3, 6, 2, D), BF),
            pltpu.VMEM((TOK, D), F32),
            pltpu.VMEM((2, 2, 8, 64, TOK), BF),
            pltpu.VMEM((2, 8, 64, TOK), BF),
            pltpu.VMEM((TOK, 1536), BF),
            pltpu.VMEM((TOK, HD), BF),
            pltpu.VMEM((8, TOK, TOK), F32),
            pltpu.VMEM((4, TOK, HD), BF),
            pltpu.VMEM((4, TOK, HD), BF),
            pltpu.VMEM((4, 4, 4, 32, HD), BF),
            pltpu.VMEM((4, 3, 4, 32, HD), BF),
            pltpu.VMEM((4, 4, 32, HD), BF),
            pltpu.VMEM((4, 3, 32, HD), BF),
            pltpu.VMEM((2, 8, 4, 2 * HD), BF),
            pltpu.VMEM((2, 7, 4, 2 * HD), BF),
            pltpu.VMEM((5, 2, D), F32),
            pltpu.VMEM((2, D), F32),
            pltpu.VMEM((2, 3, 2, D), F32),
            pltpu.VMEM((7, 2, D), F32),
            pltpu.VMEM((4, 3, 6, 2, D), BF),
            pltpu.VMEM((4, 3, 6, 2, D), BF),
            dma((8,)),
            dma((4, 3)),
            dma((4, 3)),
            dma((6,)),
            dma((6,)),
            dma((4, 3)),
            dma((4, 3)),
            dma((4, 3)),
            dma((4, 3)),
            dma((2, 7)),
            dma((2, 7)),
            dma((14,)),
            dma((14,)),
        ],
        compiler_params=pltpu.CompilerParams(
            collective_id=0, has_side_effects=True, vmem_limit_bytes=56 << 20
        ),
        name="window_step",
    )(
        tokens.transpose(1, 2, 0, 3),
        output_cotangent.transpose(1, 2, 0, 3),
        layer_norm_gain.reshape(1, D),
        layer_norm_bias.reshape(1, D),
        w_qkv,
        w_out,
    )
    small = jax.ShapeDtypeStruct((1, 4), F32)
    y_out, token_gradient, d_qkv, d_out, gain_gradient, d_bias = pl.pallas_call(
        finish,
        out_shape=(grid, grid, d_qkv_shape, d_out_shape, small, small),
        in_specs=[vmem] * 5,
        out_specs=(anywhere, anywhere, anywhere, anywhere, vmem, vmem),
        scratch_shapes=[dma((4,))],
        name="hand_out",
    )(*[pltpu.with_memory_space_constraint(r, pltpu.VMEM) for r in results])
    return (
        y_out.transpose(2, 0, 1, 3),
        token_gradient.transpose(2, 0, 1, 3),
        d_qkv,
        d_out.T,
        gain_gradient.reshape(4),
        d_bias.reshape(4),
    )


def solution(mesh):
    in_specs = (P(None, "lat", "lon", None), P(), P(), P(), P(), P(None, "lat", "lon", None))
    out_specs = (
        P(None, "lat", "lon", None),
        P(None, "lat", "lon", None),
        P(("lat", "lon"), None),
        P(None, ("lat", "lon")),
        P(("lat", "lon")),
        P(("lat", "lon")),
    )
    return jax.shard_map(
        on_device, mesh=mesh, in_specs=in_specs, out_specs=out_specs, check_vma=False
    )
```

```python
import math

import jax
import jax.numpy as jnp
from jax import lax
from jax.experimental import pallas as pl
from jax.experimental.pallas import tpu as pltpu
from jax.sharding import PartitionSpec as P

MESH = pl.DeviceIdType.MESH
BF = jnp.bfloat16
F32 = jnp.float32

D = 1024
HD = 512
TOK = 144
QUARTER = 36
NX, NY, NZ = 4, 4, 8
LAT, LON = 16, 16


def dot(a, b):
    return jnp.dot(a, b, preferred_element_type=F32)


def dot_nt(a, b):
    return lax.dot_general(a, b, (((1,), (1,)), ((), ())), preferred_element_type=F32)


def dot_tn(a, b):
    return lax.dot_general(a, b, (((0,), (0,)), ((), ())), preferred_element_type=F32)


OUT, VAL, QUE, KEY = range(4)
X_FIRST = (OUT, QUE)


def kernel(
    norm_factor,
    tok_ref,
    cot_ref,
    gain_hbm,
    bias_hbm,
    wqkv_hbm,
    wout_hbm,
    y_ref,
    tg_ref,
    dqkv_ref,
    dout_ref,
    vec_ref,
    gain_ref,
    bias_ref,
    wqkv,
    wout,
    xin,
    cin,
    xhat_s,
    left,
    left_in,
    proj,
    gatt,
    probs,
    right,
    right_in,
    part,
    one_in,
    mid,
    two_in,
    z_out,
    z_in,
    vec_out,
    vec_core,
    vec_xy,
    vec_z,
    ysend,
    tsend,
    local_sem,
    ex_send,
    ex_recv,
    core_send,
    core_recv,
    one_send,
    one_recv,
    two_send,
    two_recv,
    z_send,
    z_recv,
    vec_send,
    vec_recv,
):
    lat = lax.axis_index("lat")
    lon = lax.axis_index("lon")
    x_lo = lat // 8
    y = lax.rem(lat // 2, 4)
    core = lax.rem(lat, 2)
    x_hi = lon // 8
    z = lax.rem(lon, 8)
    x = x_hi * 2 + x_lo
    odd = core

    def wrap(v):
        return lax.rem(v + 16, 16)

    sibling = (lat + 1 - 2 * core, lon)
    along_x = []
    for s in (2, 1, 3):
        px = lax.rem(x + s, NX)
        along_x.append(((lax.rem(px, 2) * 8 + y * 2 + core, (px // 2) * 8 + z), px))
    along_y = []
    for s in (2, 1, 3):
        py = lax.rem(y + s, NY)
        along_y.append((((x_lo * 4 + py) * 2 + core, lon), py))
    along_z = []
    for s in (4, 3, 5, 2, 6, 1, 7):
        pz = lax.rem(z + s, NZ)
        along_z.append(((lat, x_hi * 8 + pz), pz))

    send_to = [
        ((wrap(lat + 1), wrap(lon + odd)), 1, 1, 0),
        ((wrap(lat + 1), wrap(lon - 1 + odd)), 1, 0, 1),
        ((lat, wrap(lon + 1 - 2 * odd)), 0, 1 - odd, 2 + odd),
    ]
    give_back = [
        ((wrap(lat - 1), wrap(lon - 1 + odd)), 1, 1, 0),
        ((wrap(lat - 1), wrap(lon + odd)), 1, 0, 1),
        ((lat, wrap(lon - 1 + 2 * odd)), 0, 1 - odd, 2 + odd),
    ]
    unsent = []

    def push(src, dst, send_sem, recv_sem, peer):
        copy = pltpu.make_async_remote_copy(
            src_ref=src,
            dst_ref=dst,
            send_sem=send_sem,
            recv_sem=recv_sem,
            device_id=peer,
            device_id_type=MESH,
        )
        copy.start()
        unsent.append(copy)
        return copy

    def arrived(copies):
        for copy in copies:
            copy.wait_recv()

    load_wqkv = pltpu.make_async_copy(wqkv_hbm, wqkv, local_sem.at[0])
    load_wout = pltpu.make_async_copy(wout_hbm, wout, local_sem.at[1])
    load_gain = pltpu.make_async_copy(gain_hbm, gain_ref, local_sem.at[6])
    load_bias = pltpu.make_async_copy(bias_hbm, bias_ref, local_sem.at[7])

    barrier = pltpu.get_barrier_semaphore()
    friends = [p[0] for p in send_to + give_back + along_z + along_x + along_y] + [sibling]
    for peer in friends:
        pl.semaphore_signal(barrier, inc=1, device_id=peer, device_id_type=MESH)

    def quarter(ref, row_half, col_half):
        return ref.at[pl.ds(3 * row_half, 3), pl.ds(6 * col_half, 6)]

    own_x = pltpu.make_async_copy(quarter(tok_ref, 0, odd), xin.at[3 - odd], local_sem.at[2])
    own_c = pltpu.make_async_copy(quarter(cot_ref, 0, odd), cin.at[3 - odd], local_sem.at[3])
    own_x.start()
    load_gain.start()
    load_bias.start()
    load_wqkv.start()
    own_c.start()
    load_wout.start()
    pl.semaphore_wait(barrier, len(friends))

    enter = []
    for kind, (src, dst) in enumerate(((tok_ref, xin), (cot_ref, cin))):
        enter.append(
            [
                push(
                    quarter(src, rh, ch),
                    dst.at[slot],
                    ex_send.at[kind, m],
                    ex_recv.at[kind, m],
                    peer,
                )
                for m, (peer, rh, ch, slot) in enumerate(send_to)
            ]
        )

    def share_left(kind, value):
        rows = value.reshape(8, 2, 64, TOK)
        for c in range(2):
            for t in range(8):
                left[kind, c, t] = rows[t, c]
        return push(
            left.at[kind, 1 - core],
            left_in.at[kind],
            core_send.at[kind],
            core_recv.at[kind],
            sibling,
        )

    own_x.wait()
    load_gain.wait()
    load_bias.wait()
    arrived(enter[0])
    tokens = xin[...].reshape(TOK, D).astype(F32)
    centered = tokens - jnp.mean(tokens, axis=-1, keepdims=True)
    inverse = lax.rsqrt(jnp.mean(centered * centered, axis=-1, keepdims=True) + 1e-05)
    xhat = centered * inverse
    xhat_s[...] = xhat
    normed = (xhat * gain_ref[...] + bias_ref[...]).astype(BF)
    load_wqkv.wait()
    proj[...] = dot(normed, wqkv[...]).astype(BF)

    slot_q = lax.broadcasted_iota(jnp.int32, (TOK, TOK), 0) // QUARTER
    slot_k = lax.broadcasted_iota(jnp.int32, (TOK, TOK), 1) // QUARTER
    lat_edge = (lat == 0).astype(jnp.int32)
    lon_edge = (lon == odd * (LON - 1)).astype(jnp.int32)
    apart = lat_edge * jnp.abs(slot_q // 2 - slot_k // 2) + lon_edge * jnp.abs(
        lax.rem(slot_q, 2) - lax.rem(slot_k, 2)
    )
    valid = apart == 0
    lane = lax.broadcasted_iota(jnp.int32, (TOK, 128), 1)
    low = lane < 64
    halves = (low.astype(F32).astype(BF), (1.0 - low.astype(F32)).astype(BF))

    def share_right(chunk):
        return push(
            right.at[chunk],
            right_in.at[chunk],
            core_send.at[2 + chunk],
            core_recv.at[2 + chunk],
            sibling,
        )

    def columns(pair):
        at = slice(pair * 128, pair * 128 + 128)
        q2 = proj[:, at]
        k2 = proj[:, 512 + pair * 128 : 640 + pair * 128]
        v2 = proj[:, 1024 + pair * 128 : 1152 + pair * 128]
        return at, q2, k2, v2

    def forward(pair):
        at, q2, k2, v2 = columns(pair)
        mixed = []
        for h, half in enumerate(halves):
            scores = jnp.where(valid, dot_nt(k2 * half, q2) * 0.125, -1e30)
            top = jnp.max(scores, axis=0, keepdims=True)
            e = jnp.exp(scores - top)
            p = e * (1.0 / jnp.sum(e, axis=0, keepdims=True))
            probs[pair * 2 + h] = p
            mixed.append(dot_tn(p.astype(BF), v2 * half))
        right[OUT, :, at] = (mixed[0] + mixed[1]).astype(BF)

    def value_gradient(pair):
        at = slice(pair * 128, pair * 128 + 128)
        g2 = gatt[:, at]
        grad_v = [dot(probs[pair * 2 + h].astype(BF), g2) for h in range(2)]
        right[VAL, :, at] = jnp.where(low, grad_v[0], grad_v[1]).astype(BF)

    def backward(pair):
        at, q2, k2, v2 = columns(pair)
        g2 = gatt[:, at]
        grad_q = []
        grad_k = []
        for h, half in enumerate(halves):
            p = probs[pair * 2 + h]
            gp = dot_nt(v2 * half, g2)
            inner = jnp.sum(p * gp, axis=0, keepdims=True)
            gs = (p * (gp - inner)).astype(BF)
            grad_q.append(dot_tn(gs, k2 * half))
            grad_k.append(dot(gs, q2))
        right[QUE, :, at] = ((grad_q[0] + grad_q[1]) * 0.125).astype(BF)
        right[KEY, :, at] = (jnp.where(low, grad_k[0], grad_k[1]) * 0.125).astype(BF)

    def first_step(chunk):
        kind = 1 if chunk == OUT else 0
        x_first = chunk in X_FIRST
        right_copies[chunk].wait_recv()
        mine = right[chunk]
        other = right_in[chunk]
        for block in range(2):
            at = slice(block * 4, block * 4 + 4)
            rows = dot(left[kind, core, at].reshape(256, TOK), mine) + dot(
                left_in[kind, at].reshape(256, TOK), other
            )
            rows = rows.astype(BF).reshape(4, 2, 32, 512)
            for t in range(4):
                for hi in range(2):
                    gx = hi * 2 + block
                    if x_first:
                        part[chunk, gx, t] = rows[t, hi]
                    else:
                        part[chunk, t, gx] = rows[t, hi]
        return [
            push(
                part.at[chunk, place],
                one_in.at[chunk, n],
                one_send.at[chunk, n],
                one_recv.at[chunk, n],
                peer,
            )
            for n, (peer, place) in enumerate(along_x if x_first else along_y)
        ]

    def second_step(chunk, copies):
        x_first = chunk in X_FIRST
        arrived(copies)
        total = part[chunk, x if x_first else y].astype(F32)
        for n in range(3):
            total = total + one_in[chunk, n].astype(F32)
        mid[chunk] = total.astype(BF)
        return [
            push(
                mid.at[chunk, place],
                two_in.at[chunk, n],
                two_send.at[chunk, n],
                two_recv.at[chunk, n],
                peer,
            )
            for n, (peer, place) in enumerate(along_y if x_first else along_x)
        ]

    def third_step(phase, pair):
        for col, (chunk, copies) in enumerate(pair):
            arrived(copies)
            total = mid[chunk, y if chunk in X_FIRST else x].astype(F32)
            for n in range(3):
                total = total + two_in[chunk, n].astype(F32)
            z_out[phase, :, :, col * 512 : col * 512 + 512] = total.astype(BF).reshape(8, 4, 512)
        return [
            push(
                z_out.at[phase, place],
                z_in.at[phase, n],
                z_send.at[phase, n],
                z_recv.at[phase, n],
                peer,
            )
            for n, (peer, place) in enumerate(along_z)
        ]

    def last_step(phase, copies):
        arrived(copies)
        total = z_out[phase, z].astype(F32)
        for n in range(7):
            total = total + z_in[phase, n].astype(F32)
        return total * norm_factor

    def start_back(kind, src, dst):
        for m, (peer, rh, ch, slot) in enumerate(give_back):
            back.append(
                push(
                    src.at[slot],
                    quarter(dst, rh, ch),
                    ex_send.at[kind, m],
                    ex_recv.at[kind, m],
                    peer,
                )
            )
        own = pltpu.make_async_copy(src.at[3 - odd], quarter(dst, 0, odd), local_sem.at[2 + kind])
        own.start()
        return own

    back = []
    for pair in range(4):
        forward(pair)
    right_copies = [share_right(OUT)]
    own_c.wait()
    arrived(enter[1])
    load_wout.wait()
    cot = cin[...].reshape(TOK, D)
    left_c = share_left(1, cot.T)
    gatt[...] = dot_nt(cot, wout[...]).astype(BF)
    for pair in range(4):
        value_gradient(pair)
    right_copies.append(share_right(VAL))
    left_n = share_left(0, normed.T)
    mixed_out = dot(right[OUT], wout[...])
    y_out = (xin[...].reshape(TOK, D).astype(F32) + mixed_out).astype(BF)
    ysend[...] = y_out.reshape(4, 3, 6, 2, D)
    own_y = start_back(3, ysend, y_ref)
    left_c.wait_recv()
    one_out = first_step(OUT)
    left_n.wait_recv()
    one_val = first_step(VAL)
    backward(0)
    backward(1)
    backward(2)
    backward(3)
    right_copies += [share_right(QUE), share_right(KEY)]

    gn = dot_nt(right[QUE], wqkv[:, 0:512])
    gn = gn + dot_nt(right[KEY], wqkv[:, 512:1024])
    gn = gn + dot_nt(right[VAL], wqkv[:, 1024:1536])
    xh = xhat_s[...]
    vec_out[0, 0:1, :] = jnp.sum(gn * xh, axis=0, keepdims=True)
    vec_out[0, 1:2, :] = jnp.sum(gn, axis=0, keepdims=True)
    vec_0 = push(vec_out.at[0], vec_core, vec_send.at[0], vec_recv.at[0], sibling)
    one_que = first_step(QUE)
    one_key = first_step(KEY)
    gh = gn * gain_ref[...]
    first = jnp.mean(gh, axis=-1, keepdims=True)
    second = jnp.mean(gh * xh, axis=-1, keepdims=True)
    cot_wide = cin[...].reshape(TOK, D).astype(F32)
    tg = (cot_wide + (gh - first - xh * second) * inverse).astype(BF)
    tsend[...] = tg.reshape(4, 3, 6, 2, D)

    def vec_step(stage, total, peers, landing, first_sem):
        vec_out[stage] = total
        return [
            push(
                vec_out.at[stage],
                landing.at[n],
                vec_send.at[first_sem + n],
                vec_recv.at[first_sem + n],
                peer[0],
            )
            for n, peer in enumerate(peers)
        ]

    vec_0.wait_recv()
    vec_1 = vec_step(1, vec_out[0] + vec_core[...], along_x, vec_xy.at[0], 1)

    two_out = second_step(OUT, one_out)
    two_val = second_step(VAL, one_val)
    two_que = second_step(QUE, one_que)
    two_key = second_step(KEY, one_key)
    arrived(vec_1)
    total = vec_out[1]
    for n in range(3):
        total = total + vec_xy[0, n]
    vec_2 = vec_step(2, total, along_y, vec_xy.at[1], 4)
    own_t = start_back(2, tsend, tg_ref)
    z_first = third_step(0, ((OUT, two_out), (VAL, two_val)))
    arrived(vec_2)
    total = vec_out[2]
    for n in range(3):
        total = total + vec_xy[1, n]
    vec_3 = vec_step(3, total, along_z, vec_z, 7)
    z_second = third_step(1, ((QUE, two_que), (KEY, two_key)))

    last_sends = z_second + vec_3
    for copy in unsent[: len(unsent) - len(last_sends)]:
        copy.wait_send()
    arrived(back)
    own_t.wait()
    own_y.wait()
    done = last_step(0, z_first)
    dout_ref[...] = done[:, 0:512]
    dqkv_ref[:, 1024:1536] = done[:, 512:1024]
    arrived(vec_3)
    total = vec_out[3]
    for n in range(7):
        total = total + vec_z[n]
    place = lat * LON + lon
    vec_out[4] = total * norm_factor
    lanes = vec_out[4, :, pl.ds(pl.multiple_of((place // 32) * 128, 128), 128)]
    vec_ref[...] = pltpu.roll(lanes, 128 - 4 * lax.rem(place, 32), 1)
    done = last_step(1, z_second)
    dqkv_ref[:, 0:1024] = done
    for copy in last_sends:
        copy.wait_send()


def finish(y_in, tg_in, dqkv_in, dout_in, vec_in, y_out, tg_out, dqkv_out, dout_out, gain_out, bias_out, sems):
    copies = [
        pltpu.make_async_copy(src, dst, sems.at[n])
        for n, (src, dst) in enumerate(
            ((y_in, y_out), (tg_in, tg_out), (dqkv_in, dqkv_out), (dout_in, dout_out))
        )
    ]
    for copy in copies:
        copy.start()
    gain_out[...] = vec_in[0:1, 0:4]
    bias_out[...] = vec_in[1:2, 0:4]
    for copy in copies:
        copy.wait()


def on_device(tokens, layer_norm_gain, layer_norm_bias, w_qkv, w_out, output_cotangent):
    total_tokens = tokens.shape[0] * tokens.shape[1] * tokens.shape[2] * LAT * LON
    norm_factor = 1.0 / math.sqrt(total_tokens)
    grid = jax.ShapeDtypeStruct((6, 12, 2, D), BF)
    d_qkv_shape = jax.ShapeDtypeStruct((4, 1536), F32)
    d_out_shape = jax.ShapeDtypeStruct((4, HD), F32)
    anywhere = pl.BlockSpec(memory_space=pl.ANY)
    vmem = pl.BlockSpec(memory_space=pltpu.VMEM)
    dma = pltpu.SemaphoreType.DMA

    def body(*refs):
        kernel(norm_factor, *refs)

    results = pl.pallas_call(
        body,
        out_shape=(
            pltpu.VMEM((6, 12, 2, D), BF),
            pltpu.VMEM((6, 12, 2, D), BF),
            pltpu.VMEM((4, 1536), F32),
            pltpu.VMEM((4, HD), F32),
            pltpu.VMEM((2, 128), F32),
        ),
        in_specs=[anywhere] * 6,
        out_specs=(vmem,) * 5,
        scratch_shapes=[
            pltpu.VMEM((1, D), F32),
            pltpu.VMEM((1, D), F32),
            pltpu.VMEM((D, 1536), BF),
            pltpu.VMEM((HD, D), BF),
            pltpu.VMEM((4, 3, 6, 2, D), BF),
            pltpu.VMEM((4, 3, 6, 2, D), BF),
            pltpu.VMEM((TOK, D), F32),
            pltpu.VMEM((2, 2, 8, 64, TOK), BF),
            pltpu.VMEM((2, 8, 64, TOK), BF),
            pltpu.VMEM((TOK, 1536), BF),
            pltpu.VMEM((TOK, HD), BF),
            pltpu.VMEM((8, TOK, TOK), F32),
            pltpu.VMEM((4, TOK, HD), BF),
            pltpu.VMEM((4, TOK, HD), BF),
            pltpu.VMEM((4, 4, 4, 32, HD), BF),
            pltpu.VMEM((4, 3, 4, 32, HD), BF),
            pltpu.VMEM((4, 4, 32, HD), BF),
            pltpu.VMEM((4, 3, 32, HD), BF),
            pltpu.VMEM((2, 8, 4, 2 * HD), BF),
            pltpu.VMEM((2, 7, 4, 2 * HD), BF),
            pltpu.VMEM((5, 2, D), F32),
            pltpu.VMEM((2, D), F32),
            pltpu.VMEM((2, 3, 2, D), F32),
            pltpu.VMEM((7, 2, D), F32),
            pltpu.VMEM((4, 3, 6, 2, D), BF),
            pltpu.VMEM((4, 3, 6, 2, D), BF),
            dma((8,)),
            dma((4, 3)),
            dma((4, 3)),
            dma((6,)),
            dma((6,)),
            dma((4, 3)),
            dma((4, 3)),
            dma((4, 3)),
            dma((4, 3)),
            dma((2, 7)),
            dma((2, 7)),
            dma((14,)),
            dma((14,)),
        ],
        compiler_params=pltpu.CompilerParams(
            collective_id=0, has_side_effects=True, vmem_limit_bytes=56 << 20
        ),
        name="window_step",
    )(
        tokens.transpose(1, 2, 0, 3),
        output_cotangent.transpose(1, 2, 0, 3),
        layer_norm_gain.reshape(1, D),
        layer_norm_bias.reshape(1, D),
        w_qkv,
        w_out,
    )
    small = jax.ShapeDtypeStruct((1, 4), F32)
    y_out, token_gradient, d_qkv, d_out, gain_gradient, d_bias = pl.pallas_call(
        finish,
        out_shape=(grid, grid, d_qkv_shape, d_out_shape, small, small),
        in_specs=[vmem] * 5,
        out_specs=(anywhere, anywhere, anywhere, anywhere, vmem, vmem),
        scratch_shapes=[dma((4,))],
        name="hand_out",
    )(*[pltpu.with_memory_space_constraint(r, pltpu.VMEM) for r in results])
    return (
        y_out.transpose(2, 0, 1, 3),
        token_gradient.transpose(2, 0, 1, 3),
        d_qkv,
        d_out.T,
        gain_gradient.reshape(4),
        d_bias.reshape(4),
    )


def solution(mesh):
    in_specs = (P(None, "lat", "lon", None), P(), P(), P(), P(), P(None, "lat", "lon", None))
    out_specs = (
        P(None, "lat", "lon", None),
        P(None, "lat", "lon", None),
        P(("lat", "lon"), None),
        P(None, ("lat", "lon")),
        P(("lat", "lon")),
        P(("lat", "lon")),
    )
    return jax.shard_map(
        on_device, mesh=mesh, in_specs=in_specs, out_specs=out_specs, check_vma=False
    )
```
